32 devices in a mesh: px: 8 (over z, core), py: 4 (over y, x).
Axes of the slice: x: 2, y: 2, z: 4, core: 2. Of those that a mesh axis runs over, the one named last changes fastest.
Arguments:
- initial_heat_state: float32 [4, 1024, 1024], P(None, 'px', 'py'), may hold values from -6 to 7
- spreading_coefficient: float32 [4, 1024, 1024], P(None, 'px', 'py'), may hold values from 0.5 to 200000, as said below
Outputs:
- heat: float32 [4, 1024, 1024], P(None, 'px', 'py')
The draws below stay inside these ranges and needn't reach their ends.
Inputs may be any that keep to these rules, and one draw needn't show every extreme that they name: `spreading_coefficient`: positive in every cell.
All inputs are finite; a program needn't handle non-finite values.
Results may differ from the reference program's by a relative error of at most 0.0004.
Values sent between devices are 32-bit elements; how exact they have to be, the bound alone decides.
A program may use at most 64 MiB of HBM per device.

```python
import jax
import jax.numpy as jnp
from jax import lax

NX = 1024
NY = 1024
NZ = 4


def draw_spreading_coefficient(key, part):
    plane_key = jax.random.fold_in(key, 11)
    cell_key = jax.random.fold_in(key, 12)
    plane = 10.0 ** (5.0 * jax.random.uniform(plane_key, (NZ, 1, 1), jnp.float32))
    cell = 2.0 ** jax.random.uniform(cell_key, (NZ, NX, NY), jnp.float32, -1.0, 1.0)
    return (plane * cell).astype(jnp.float32)


def draw_initial_heat_state(key, part):
    rough_key = jax.random.fold_in(key, 21)
    along_x = jnp.sin(jnp.pi * (jnp.arange(NX).astype(jnp.float32) + 0.5) / NX)
    vertical_sweep_output = jnp.sin(jnp.pi * (jnp.arange(NY).astype(jnp.float32) + 0.5) / NY)
    smooth = along_x[None, :, None] * vertical_sweep_output[None, None, :]
    rough = jnp.clip(jax.random.normal(rough_key, (NZ, NX, NY), jnp.float32), -5.0, 5.0)
    result = rough + smooth
    return result.astype(jnp.float32)


def setup_inputs(seed: int = 0) -> dict:
    arg_keys = jax.random.split(jax.random.key(seed), 3)
    return {
        "initial_heat_state": draw_initial_heat_state(jax.random.fold_in(arg_keys[2], 71), 0),
        "spreading_coefficient": draw_spreading_coefficient(jax.random.fold_in(arg_keys[2], 71), 0),
    }


def thomas_algorithm(spreading_coefficient, source):
    lower = (-spreading_coefficient).at[0].set(0.0)
    upper = (-spreading_coefficient).at[-1].set(0.0)
    middle = 1.0 + 2.0 * spreading_coefficient
    zero = jnp.zeros(source.shape[1:], source.dtype)

    def forward(carry, inputs):
        ratio, value = carry
        low_now, mid_now, up_now, src_now = inputs
        divisor = mid_now - low_now * ratio
        ratio_new = up_now / divisor
        value_new = (src_now - low_now * value) / divisor
        return (ratio_new, value_new), (ratio_new, value_new)

    carried, (ratios, value_field) = lax.scan(forward, (zero, zero), (lower, middle, upper, source))

    def backward(later, inputs):
        ratio, value = inputs
        now = value - ratio * later
        return now, now

    carried, solved = lax.scan(backward, zero, (ratios, value_field), reverse=True)
    return solved


def reference(initial_heat_state, spreading_coefficient):
    padded_margin_grid = jnp.pad(initial_heat_state, 1)
    center = padded_margin_grid[1:-1, 1:-1, 1:-1]
    neighbours = padded_margin_grid[2:, 1:-1, 1:-1] + padded_margin_grid[:-2, 1:-1, 1:-1]
    neighbours = neighbours + padded_margin_grid[1:-1, 2:, 1:-1] + padded_margin_grid[1:-1, :-2, 1:-1]
    neighbours = neighbours + padded_margin_grid[1:-1, 1:-1, 2:] + padded_margin_grid[1:-1, 1:-1, :-2]
    source = center + 0.125 * (neighbours - 6.0 * center)
    after_x = jnp.moveaxis(thomas_algorithm(jnp.moveaxis(spreading_coefficient, 1, 0), jnp.moveaxis(source, 1, 0)), 0, 1)
    heat = jnp.moveaxis(thomas_algorithm(jnp.moveaxis(spreading_coefficient, 2, 0), jnp.moveaxis(after_x, 2, 0)), 0, 2)
    return heat
```

```python
import functools

import jax
import jax.numpy as jnp
from jax import lax
from jax.experimental import pallas as pl
from jax.experimental.pallas import tpu as pltpu
from jax.sharding import PartitionSpec as P

LANES = 128
BLOCKS = 8
MESH = pl.DeviceIdType.MESH


def combine(left, right):
    e_p, w_p, a_p = left
    e_q, w_q, a_q = right
    gap_p = e_p + w_p
    gap_q = e_q + a_q
    r_p = 1.0 - gap_p
    b_q = 1.0 - gap_q
    inv = 1.0 / (gap_p + r_p * gap_q)
    joined = (
        e_p * e_q * inv,
        w_q + e_q * ((w_p + r_p * a_q) * inv),
        a_p + e_p * ((a_q + b_q * w_p) * inv),
    )
    return joined, (inv, r_p, b_q, e_p, e_q)


def combine_rhs(node, left, right):
    inv, r_p, b_q, e_p, e_q = node
    u_p, a_p = left
    u_q, a_q = right
    p0 = (u_p + r_p * a_q) * inv
    q0 = (a_q + b_q * u_p) * inv
    return (u_q + e_q * p0, a_p + e_p * q0), (p0, q0)


def split(node, start, low, high):
    inv, r_p, b_q, e_p, e_q = node
    p0, q0 = start
    from_low = e_p * inv * low
    from_high = e_q * inv * high
    p = p0 + from_low + r_p * from_high
    q = q0 + b_q * from_low + from_high
    return p, q


def tree_coefficients(leaves):
    nodes = []
    while len(leaves) > 1:
        pairs = [combine(leaves[i], leaves[i + 1]) for i in range(0, len(leaves), 2)]
        leaves = [pair[0] for pair in pairs]
        nodes.append([pair[1] for pair in pairs])
    return leaves[0], nodes


def tree_up(nodes, leaves):
    starts = []
    for level in nodes:
        pairs = [
            combine_rhs(level[i], leaves[2 * i], leaves[2 * i + 1]) for i in range(len(level))
        ]
        leaves = [pair[0] for pair in pairs]
        starts.append([pair[1] for pair in pairs])
    return leaves[0], starts


def tree_down(nodes, starts, low, high):
    bounds = [(low, high)]
    for level, begin in zip(reversed(nodes), reversed(starts)):
        below = []
        for i, (lo, hi) in enumerate(bounds):
            p, q = split(level[i], begin[i], lo, hi)
            below += [(lo, q), (p, hi)]
        bounds = below
    return bounds


def leaf_rows(turn_ref, values, count):
    turn_ref[0 : count * BLOCKS, :] = values.reshape(count * BLOCKS, LANES)
    return [turn_ref[pl.ds(b, count, stride=BLOCKS), :] for b in range(BLOCKS)]


def block_rows(turn_ref, rows, count):
    for b in range(BLOCKS):
        turn_ref[pl.ds(b, count, stride=BLOCKS), :] = rows[b]
    return turn_ref[0 : count * BLOCKS, :].reshape(count, BLOCKS, LANES)


def sweep_coefficients(m_ref, r_ref, e_ref, turn_refs, length):
    count = m_ref.shape[0]
    for g in range(length):
        m = m_ref[:, pl.ds(g, BLOCKS, stride=length), :]
        if g == 0:
            t = 1.0 + m
            r = 1.0 / (1.0 + t)
            e = r
            w = m * r
            a = w
        else:
            t = m + t * r
            r = 1.0 / (1.0 + t)
            w = (m + w) * r
            a = a + e * w
            e = e * r
        r_ref[g] = r
        e_ref[g] = e
    leaves = [leaf_rows(ref, value, count) for ref, value in zip(turn_refs, (e, w, a))]
    return tree_coefficients([tuple(leaf[b] for leaf in leaves) for b in range(BLOCKS)])


def chain_coefficients(gathered, count):
    blocks = [tuple(gathered[i, c] for c in range(3)) for i in range(count)]
    total, nodes = blocks[0], []
    for i in range(1, count):
        total, node = combine(total, blocks[i])
        nodes.append(node)
    return nodes


def chain_solve(nodes, gathered, last_ref, first_ref, count):
    u = [gathered[i, 0] for i in range(count)]
    a = [gathered[i, 1] for i in range(count)]
    zero = jnp.zeros_like(u[0])
    state = (u[0], zero)
    starts = []
    for i in range(1, count):
        state, start = combine_rhs(nodes[i - 1], state, (u[i], a[i]))
        starts.append(start)
    last_ref[0] = zero
    first_ref[count - 1] = zero
    high = zero
    for i in range(count - 1, 0, -1):
        p, q = split(nodes[i - 1], starts[i - 1], zero, high)
        last_ref[i] = p
        first_ref[i - 1] = q
        high = q


def kernel(
    nx,
    ny,
    h_ref,
    k_ref,
    out_ref,
    m_ref,
    mt_ref,
    rx_ref,
    ex_ref,
    ux_ref,
    ry_ref,
    ey_ref,
    uy_ref,
    mid_ref,
    midt_ref,
    turn0,
    turn1,
    turn2,
    hxs_ref,
    hxr_ref,
    hys_ref,
    hyr_ref,
    col_ref,
    cgx,
    rgx,
    cgy,
    rgy,
    lastx,
    firstx,
    lasty,
    firsty,
    hs_sem,
    hr_sem,
    csx,
    crx,
    rsx,
    rrx,
    csy,
    cry,
    rsy,
    rry,
):
    ix = lax.axis_index("px")
    iy = lax.axis_index("py")
    planes, rows, columns = h_ref.shape
    tiles = columns // LANES
    lx = rows // BLOCKS
    ly = columns // BLOCKS
    turns = (turn0, turn1, turn2)

    barrier = pltpu.get_barrier_semaphore()
    for d in range(1, nx):
        pl.semaphore_signal(
            barrier, inc=1, device_id=(lax.rem(ix + d, nx), iy), device_id_type=MESH
        )
    for d in range(1, ny):
        pl.semaphore_signal(
            barrier, inc=1, device_id=(ix, lax.rem(iy + d, ny)), device_id_type=MESH
        )

    def peers_x(ref, send, recv):
        return [
            pltpu.make_async_remote_copy(
                src_ref=ref.at[ix],
                dst_ref=ref.at[ix],
                send_sem=send.at[d - 1],
                recv_sem=recv.at[d - 1],
                device_id=(lax.rem(ix + d, nx), iy),
                device_id_type=MESH,
            )
            for d in range(1, nx)
        ]

    def peers_y(ref, send, recv):
        return [
            pltpu.make_async_remote_copy(
                src_ref=ref.at[iy],
                dst_ref=ref.at[iy],
                send_sem=send.at[d - 1],
                recv_sem=recv.at[d - 1],
                device_id=(ix, lax.rem(iy + d, ny)),
                device_id_type=MESH,
            )
            for d in range(1, ny)
        ]

    for j in range(tiles):
        at = pl.ds(j * LANES, LANES)
        part = pl.ds(j * planes, planes)
        hxs_ref[0, part] = h_ref[:, 0, at]
        hxs_ref[1, part] = h_ref[:, rows - 1, at]
    lane = lax.broadcasted_iota(jnp.int32, (rows, LANES), 1)
    packed = jnp.zeros((rows, LANES), jnp.float32)
    for p in range(planes):
        low = h_ref[p, :, 0:LANES]
        high = h_ref[p, :, columns - LANES : columns]
        packed = jnp.where(lane == p, low if p == 0 else pltpu.roll(low, p, 1), packed)
        packed = jnp.where(lane == planes + p, pltpu.roll(high, planes + p + 1, 1), packed)
    edge = packed.T
    hys_ref[0] = edge[0:planes]
    hys_ref[1] = edge[planes : 2 * planes]

    @pl.when(ix == 0)
    def _():
        hxr_ref[1] = jnp.zeros_like(hxr_ref[1])

    @pl.when(ix == nx - 1)
    def _():
        hxr_ref[0] = jnp.zeros_like(hxr_ref[0])

    @pl.when(iy == 0)
    def _():
        hyr_ref[1] = jnp.zeros_like(hyr_ref[1])

    @pl.when(iy == ny - 1)
    def _():
        hyr_ref[0] = jnp.zeros_like(hyr_ref[0])

    def halo(source, target, slot, number, device):
        return pltpu.make_async_remote_copy(
            src_ref=source.at[slot],
            dst_ref=target.at[slot],
            send_sem=hs_sem.at[number],
            recv_sem=hr_sem.at[number],
            device_id=device,
            device_id_type=MESH,
        )

    x_down = halo(hxs_ref, hxr_ref, 0, 0, (lax.rem(ix + nx - 1, nx), iy))
    x_up = halo(hxs_ref, hxr_ref, 1, 1, (lax.rem(ix + 1, nx), iy))
    y_down = halo(hys_ref, hyr_ref, 0, 2, (ix, lax.rem(iy + ny - 1, ny)))
    y_up = halo(hys_ref, hyr_ref, 1, 3, (ix, lax.rem(iy + 1, ny)))
    routes = (
        (x_down, ix > 0, ix < nx - 1),
        (x_up, ix < nx - 1, ix > 0),
        (y_down, iy > 0, iy < ny - 1),
        (y_up, iy < ny - 1, iy > 0),
    )

    pl.semaphore_wait(barrier, nx + ny - 2)
    for copy, sends, _ in routes:
        pl.when(sends)(copy.start)

    for j in range(tiles):
        mid_ref[pl.ds(j * planes, planes)] = h_ref[:, :, pl.ds(j * LANES, LANES)]
        m_ref[pl.ds(j * planes, planes)] = 1.0 / k_ref[:, :, pl.ds(j * LANES, LANES)]
    joined, nodes_x = sweep_coefficients(m_ref, rx_ref, ex_ref, turns, lx)
    for c in range(3):
        cgx[ix, c] = joined[c]
    send_cx = peers_x(cgx, csx, crx)
    for copy in send_cx:
        copy.start()
    for p in range(planes):
        for j in range(tiles):
            mt_ref[p, pl.ds(j * LANES, LANES), :] = m_ref[j * planes + p].T
    joined, nodes_y = sweep_coefficients(mt_ref, ry_ref, ey_ref, turns, ly)
    for c in range(3):
        cgy[iy, c] = joined[c]
    send_cy = peers_y(cgy, csy, cry)
    for copy in send_cy:
        copy.start()

    for copy, _, receives in routes:
        pl.when(receives)(copy.wait_recv)
    spread = jnp.concatenate(
        [hyr_ref[1], hyr_ref[0], jnp.zeros((LANES - 2 * planes, LANES), jnp.float32)], axis=0
    )
    col_ref[...] = spread.T

    def field(g):
        return mid_ref[:, pl.ds(g, BLOCKS, stride=lx), :]

    count = tiles * planes
    shape = (count, BLOCKS, LANES)
    sub = lax.broadcasted_iota(jnp.int32, shape, 1)
    lane1 = lax.broadcasted_iota(jnp.int32, (BLOCKS, LANES), 1)
    none = jnp.zeros((BLOCKS, LANES), jnp.float32)
    now = field(0)
    before = jnp.where(sub == 0, hxr_ref[1][:, None, :], pltpu.roll(field(lx - 1), 1, 1))
    beyond = jnp.where(sub == BLOCKS - 1, hxr_ref[0][:, None, :], pltpu.roll(now, BLOCKS - 1, 1))
    u = jnp.zeros(shape, jnp.float32)
    total = jnp.zeros(shape, jnp.float32)
    for g in range(lx):
        after = field(g + 1) if g + 1 < lx else beyond
        to_right = pltpu.roll(now, 1, 2)
        to_left = pltpu.roll(now, LANES - 1, 2)
        column = col_ref[pl.ds(g, BLOCKS, stride=lx), :]
        around = []
        for j in range(tiles):
            for p in range(planes):
                i = j * planes + p
                if j == 0:
                    low = column if p == 0 else pltpu.roll(column, LANES - p, 1)
                else:
                    low = to_right[i - planes]
                if j == tiles - 1:
                    high = pltpu.roll(column, LANES - 1 - planes - p, 1)
                else:
                    high = to_left[i + planes]
                left = jnp.where(lane1 == 0, low, to_right[i])
                right = jnp.where(lane1 == LANES - 1, high, to_left[i])
                under = now[i - 1] if p > 0 else none
                over = now[i + 1] if p < planes - 1 else none
                around.append((over + under) + (left + right))
        around = jnp.stack(around) + (after + before)
        source = now + 0.125 * (around - 6.0 * now)
        m = m_ref[:, pl.ds(g, BLOCKS, stride=lx), :]
        u = (source * m + u) * rx_ref[g]
        total = u if g == 0 else total + ex_ref[g - 1] * u
        ux_ref[g] = u
        before, now = now, after

    def finish_sweep(u, total, nodes, count, length, r_ref, e_ref, u_ref, store, exchange):
        leaves = [leaf_rows(ref, value, count) for ref, value in zip(turns, (u, total))]
        (u_top, a_top), starts = tree_up(nodes, list(zip(*leaves)))
        low, high = exchange(u_top, a_top)
        bounds = tree_down(nodes, starts, low, high)
        low = block_rows(turn0, [b[0] for b in bounds], count)
        value = block_rows(turn1, [b[1] for b in bounds], count)
        for g in range(length - 1, -1, -1):
            value = (u_ref[g] + e_ref[g] * low) + r_ref[g] * value
            store(g, value)

    def exchange_x(u_top, a_top):
        rgx[ix, 0] = u_top
        rgx[ix, 1] = a_top
        send = peers_x(rgx, rsx, rrx)
        for copy in send:
            copy.start()
        for copy in send_cx:
            copy.wait()
        chain = chain_coefficients(cgx, nx)
        for copy in send:
            copy.wait()
        chain_solve(chain, rgx, lastx, firstx, nx)
        return lastx[ix], firstx[ix]

    def exchange_y(u_top, a_top):
        rgy[iy, 0] = u_top
        rgy[iy, 1] = a_top
        send = peers_y(rgy, rsy, rry)
        for copy in send:
            copy.start()
        for copy in send_cy:
            copy.wait()
        chain = chain_coefficients(cgy, ny)
        for copy in send:
            copy.wait()
        chain_solve(chain, rgy, lasty, firsty, ny)
        return lasty[iy], firsty[iy]

    def store_x(g, value):
        mid_ref[:, pl.ds(g, BLOCKS, stride=lx), :] = value

    finish_sweep(u, total, nodes_x, count, lx, rx_ref, ex_ref, ux_ref, store_x, exchange_x)

    for p in range(planes):
        for j in range(tiles):
            midt_ref[p, pl.ds(j * LANES, LANES), :] = mid_ref[j * planes + p].T
    u = jnp.zeros((planes, BLOCKS, LANES), jnp.float32)
    total = u
    for g in range(ly):
        source = midt_ref[:, pl.ds(g, BLOCKS, stride=ly), :]
        m = mt_ref[:, pl.ds(g, BLOCKS, stride=ly), :]
        u = (source * m + u) * ry_ref[g]
        total = u if g == 0 else total + ey_ref[g - 1] * u
        uy_ref[g] = u

    def store_y(g, value):
        midt_ref[:, pl.ds(g, BLOCKS, stride=ly), :] = value

    finish_sweep(u, total, nodes_y, planes, ly, ry_ref, ey_ref, uy_ref, store_y, exchange_y)
    for p in range(planes):
        for j in range(tiles):
            at = pl.ds(j * LANES, LANES)
            out_ref[p, :, at] = midt_ref[p, at, :].T
    for copy, sends, _ in routes:
        pl.when(sends)(copy.wait_send)


def on_device(nx, ny, initial_heat_state, spreading_coefficient):
    planes, rows, columns = initial_heat_state.shape
    count = planes * (columns // LANES)
    lx = rows // BLOCKS
    ly = columns // BLOCKS

    def vmem(*shape):
        return pltpu.VMEM(shape, jnp.float32)

    def dma(number):
        return pltpu.SemaphoreType.DMA((number,))

    return pl.pallas_call(
        functools.partial(kernel, nx, ny),
        out_shape=jax.ShapeDtypeStruct((planes, rows, columns), jnp.float32),
        in_specs=[pl.BlockSpec(memory_space=pltpu.VMEM)] * 2,
        out_specs=pl.BlockSpec(memory_space=pltpu.VMEM),
        scratch_shapes=[
            vmem(count, rows, LANES),
            vmem(planes, columns, LANES),
            vmem(lx, count, BLOCKS, LANES),
            vmem(lx, count, BLOCKS, LANES),
            vmem(lx, count, BLOCKS, LANES),
            vmem(ly, planes, BLOCKS, LANES),
            vmem(ly, planes, BLOCKS, LANES),
            vmem(ly, planes, BLOCKS, LANES),
            vmem(count, rows, LANES),
            vmem(planes, columns, LANES),
            vmem(count * BLOCKS, LANES),
            vmem(count * BLOCKS, LANES),
            vmem(count * BLOCKS, LANES),
            vmem(2, count, LANES),
            vmem(2, count, LANES),
            vmem(2, planes, LANES),
            vmem(2, planes, LANES),
            vmem(rows, LANES),
            vmem(nx, 3, count, LANES),
            vmem(nx, 2, count, LANES),
            vmem(ny, 3, planes, LANES),
            vmem(ny, 2, planes, LANES),
            vmem(nx, count, LANES),
            vmem(nx, count, LANES),
            vmem(ny, planes, LANES),
            vmem(ny, planes, LANES),
            dma(4),
            dma(4),
            dma(nx - 1),
            dma(nx - 1),
            dma(nx - 1),
            dma(nx - 1),
            dma(ny - 1),
            dma(ny - 1),
            dma(ny - 1),
            dma(ny - 1),
        ],
        compiler_params=pltpu.CompilerParams(
            collective_id=0, has_side_effects=True, vmem_limit_bytes=32 << 20
        ),
    )(initial_heat_state, spreading_coefficient)


def solution(mesh):
    return jax.shard_map(
        functools.partial(on_device, mesh.shape["px"], mesh.shape["py"]),
        mesh=mesh,
        in_specs=(P(None, "px", "py"), P(None, "px", "py")),
        out_specs=P(None, "px", "py"),
        check_vma=False,
    )
```

```python
import functools

import jax
import jax.numpy as jnp
from jax import lax
from jax.experimental import pallas as pl
from jax.experimental.pallas import tpu as pltpu
from jax.sharding import PartitionSpec as P

LANES = 128
BLOCKS = 8
MESH = pl.DeviceIdType.MESH


def combine(left, right):
    e_p, w_p, a_p = left
    e_q, w_q, a_q = right
    gap_p = e_p + w_p
    gap_q = e_q + a_q
    r_p = 1.0 - gap_p
    b_q = 1.0 - gap_q
    inv = 1.0 / (gap_p + r_p * gap_q)
    joined = (
        e_p * e_q * inv,
        w_q + e_q * ((w_p + r_p * a_q) * inv),
        a_p + e_p * ((a_q + b_q * w_p) * inv),
    )
    return joined, (inv, r_p, b_q, e_p, e_q)


def combine_rhs(node, left, right):
    inv, r_p, b_q, e_p, e_q = node
    u_p, a_p = left
    u_q, a_q = right
    p0 = (u_p + r_p * a_q) * inv
    q0 = (a_q + b_q * u_p) * inv
    return (u_q + e_q * p0, a_p + e_p * q0), (p0, q0)


def split(node, start, low, high):
    inv, r_p, b_q, e_p, e_q = node
    p0, q0 = start
    from_low = e_p * inv * low
    from_high = e_q * inv * high
    p = p0 + from_low + r_p * from_high
    q = q0 + b_q * from_low + from_high
    return p, q


def tree_coefficients(leaves):
    nodes = []
    while len(leaves) > 1:
        pairs = [combine(leaves[i], leaves[i + 1]) for i in range(0, len(leaves), 2)]
        leaves = [pair[0] for pair in pairs]
        nodes.append([pair[1] for pair in pairs])
    return leaves[0], nodes


def tree_up(nodes, leaves):
    starts = []
    for level in nodes:
        pairs = [
            combine_rhs(level[i], leaves[2 * i], leaves[2 * i + 1]) for i in range(len(level))
        ]
        leaves = [pair[0] for pair in pairs]
        starts.append([pair[1] for pair in pairs])
    return leaves[0], starts


def tree_down(nodes, starts, low, high):
    bounds = [(low, high)]
    for level, begin in zip(reversed(nodes), reversed(starts)):
        below = []
        for i, (lo, hi) in enumerate(bounds):
            p, q = split(level[i], begin[i], lo, hi)
            below += [(lo, q), (p, hi)]
        bounds = below
    return bounds


def leaf_rows(turn_ref, values, count):
    turn_ref[0 : count * BLOCKS, :] = values.reshape(count * BLOCKS, LANES)
    return [turn_ref[pl.ds(b, count, stride=BLOCKS), :] for b in range(BLOCKS)]


def block_rows(turn_ref, rows, count):
    for b in range(BLOCKS):
        turn_ref[pl.ds(b, count, stride=BLOCKS), :] = rows[b]
    return turn_ref[0 : count * BLOCKS, :].reshape(count, BLOCKS, LANES)


def sweep_coefficients(m_ref, r_ref, e_ref, turn_refs, length):
    count = m_ref.shape[0]
    for g in range(length):
        m = m_ref[:, pl.ds(g, BLOCKS, stride=length), :]
        if g == 0:
            t = 1.0 + m
            r = 1.0 / (1.0 + t)
            e = r
            w = m * r
            a = w
        else:
            t = m + t * r
            r = 1.0 / (1.0 + t)
            w = (m + w) * r
            a = a + e * w
            e = e * r
        r_ref[g] = r
        e_ref[g] = e
    leaves = [leaf_rows(ref, value, count) for ref, value in zip(turn_refs, (e, w, a))]
    return tree_coefficients([tuple(leaf[b] for leaf in leaves) for b in range(BLOCKS)])


def chain_coefficients(gathered, count):
    blocks = [tuple(gathered[i, c] for c in range(3)) for i in range(count)]
    total, nodes = blocks[0], []
    for i in range(1, count):
        total, node = combine(total, blocks[i])
        nodes.append(node)
    return nodes


def chain_solve(nodes, gathered, last_ref, first_ref, count):
    u = [gathered[i, 0] for i in range(count)]
    a = [gathered[i, 1] for i in range(count)]
    zero = jnp.zeros_like(u[0])
    state = (u[0], zero)
    starts = []
    for i in range(1, count):
        state, start = combine_rhs(nodes[i - 1], state, (u[i], a[i]))
        starts.append(start)
    last_ref[0] = zero
    first_ref[count - 1] = zero
    high = zero
    for i in range(count - 1, 0, -1):
        p, q = split(nodes[i - 1], starts[i - 1], zero, high)
        last_ref[i] = p
        first_ref[i - 1] = q
        high = q


def kernel(
    nx,
    ny,
    h_hbm,
    k_hbm,
    out_ref,
    k_ref,
    m_ref,
    mt_ref,
    rx_ref,
    ex_ref,
    ux_ref,
    ry_ref,
    ey_ref,
    uy_ref,
    mid_ref,
    midt_ref,
    turn0,
    turn1,
    turn2,
    hxs_ref,
    hxr_ref,
    hys_ref,
    hyr_ref,
    col_ref,
    cgx,
    rgx,
    cgy,
    rgy,
    lastx,
    firstx,
    lasty,
    firsty,
    in_sem,
    hs_sem,
    hr_sem,
    csx,
    crx,
    rsx,
    rrx,
    csy,
    cry,
    rsy,
    rry,
):
    ix = lax.axis_index("px")
    iy = lax.axis_index("py")
    planes, rows, columns = h_hbm.shape
    tiles = columns // LANES
    lx = rows // BLOCKS
    ly = columns // BLOCKS
    turns = (turn0, turn1, turn2)

    def stage(source, target, j, number):
        return pltpu.make_async_copy(
            source.at[:, :, pl.ds(j * LANES, LANES)],
            target.at[pl.ds(j * planes, planes)],
            in_sem.at[number],
        )

    stage_k = [stage(k_hbm, k_ref, j, j) for j in range(tiles)]
    stage_h = [stage(h_hbm, mid_ref, j, tiles + j) for j in range(tiles)]
    for copy in stage_h:
        copy.start()

    barrier = pltpu.get_barrier_semaphore()
    for d in range(1, nx):
        pl.semaphore_signal(
            barrier, inc=1, device_id=(lax.rem(ix + d, nx), iy), device_id_type=MESH
        )
    for d in range(1, ny):
        pl.semaphore_signal(
            barrier, inc=1, device_id=(ix, lax.rem(iy + d, ny)), device_id_type=MESH
        )

    for copy in stage_k:
        copy.start()

    def peers_x(ref, send, recv):
        return [
            pltpu.make_async_remote_copy(
                src_ref=ref.at[ix],
                dst_ref=ref.at[ix],
                send_sem=send.at[d - 1],
                recv_sem=recv.at[d - 1],
                device_id=(lax.rem(ix + d, nx), iy),
                device_id_type=MESH,
            )
            for d in range(1, nx)
        ]

    def peers_y(ref, send, recv):
        return [
            pltpu.make_async_remote_copy(
                src_ref=ref.at[iy],
                dst_ref=ref.at[iy],
                send_sem=send.at[d - 1],
                recv_sem=recv.at[d - 1],
                device_id=(ix, lax.rem(iy + d, ny)),
                device_id_type=MESH,
            )
            for d in range(1, ny)
        ]

    @pl.when(ix == 0)
    def _():
        hxr_ref[1] = jnp.zeros_like(hxr_ref[1])

    @pl.when(ix == nx - 1)
    def _():
        hxr_ref[0] = jnp.zeros_like(hxr_ref[0])

    @pl.when(iy == 0)
    def _():
        hyr_ref[1] = jnp.zeros_like(hyr_ref[1])

    @pl.when(iy == ny - 1)
    def _():
        hyr_ref[0] = jnp.zeros_like(hyr_ref[0])

    def halo(source, target, slot, number, device):
        return pltpu.make_async_remote_copy(
            src_ref=source.at[slot],
            dst_ref=target.at[slot],
            send_sem=hs_sem.at[number],
            recv_sem=hr_sem.at[number],
            device_id=device,
            device_id_type=MESH,
        )

    x_down = halo(hxs_ref, hxr_ref, 0, 0, (lax.rem(ix + nx - 1, nx), iy))
    x_up = halo(hxs_ref, hxr_ref, 1, 1, (lax.rem(ix + 1, nx), iy))
    y_down = halo(hys_ref, hyr_ref, 0, 2, (ix, lax.rem(iy + ny - 1, ny)))
    y_up = halo(hys_ref, hyr_ref, 1, 3, (ix, lax.rem(iy + 1, ny)))
    routes = (
        (x_down, ix > 0, ix < nx - 1),
        (x_up, ix < nx - 1, ix > 0),
        (y_down, iy > 0, iy < ny - 1),
        (y_up, iy < ny - 1, iy > 0),
    )

    for copy in stage_h:
        copy.wait()
    hxs_ref[0] = mid_ref[:, 0, :]
    hxs_ref[1] = mid_ref[:, rows - 1, :]
    lane = lax.broadcasted_iota(jnp.int32, (rows, LANES), 1)
    packed = jnp.zeros((rows, LANES), jnp.float32)
    for p in range(planes):
        low = mid_ref[p]
        high = mid_ref[(tiles - 1) * planes + p]
        packed = jnp.where(lane == p, low if p == 0 else pltpu.roll(low, p, 1), packed)
        packed = jnp.where(lane == planes + p, pltpu.roll(high, planes + p + 1, 1), packed)
    edge = packed.T
    hys_ref[0] = edge[0:planes]
    hys_ref[1] = edge[planes : 2 * planes]

    pl.semaphore_wait(barrier, nx + ny - 2)
    for copy, sends, _ in routes:
        pl.when(sends)(copy.start)

    for j in range(tiles):
        part = pl.ds(j * planes, planes)
        stage_k[j].wait()
        m_ref[part] = 1.0 / k_ref[part]
    joined, nodes_x = sweep_coefficients(m_ref, rx_ref, ex_ref, turns, lx)
    for c in range(3):
        cgx[ix, c] = joined[c]
    send_cx = peers_x(cgx, csx, crx)
    for copy in send_cx:
        copy.start()
    for p in range(planes):
        for j in range(tiles):
            mt_ref[p, pl.ds(j * LANES, LANES), :] = m_ref[j * planes + p].T
    joined, nodes_y = sweep_coefficients(mt_ref, ry_ref, ey_ref, turns, ly)
    for c in range(3):
        cgy[iy, c] = joined[c]
    send_cy = peers_y(cgy, csy, cry)
    for copy in send_cy:
        copy.start()
    started = send_cx + send_cy

    for copy, _, receives in routes:
        pl.when(receives)(copy.wait_recv)
    spread = jnp.concatenate(
        [hyr_ref[1], hyr_ref[0], jnp.zeros((LANES - 2 * planes, LANES), jnp.float32)], axis=0
    )
    col_ref[...] = spread.T

    def field(g):
        return mid_ref[:, pl.ds(g, BLOCKS, stride=lx), :]

    count = tiles * planes
    shape = (count, BLOCKS, LANES)
    sub = lax.broadcasted_iota(jnp.int32, shape, 1)
    lane1 = lax.broadcasted_iota(jnp.int32, (BLOCKS, LANES), 1)
    none = jnp.zeros((BLOCKS, LANES), jnp.float32)
    now = field(0)
    before = jnp.where(sub == 0, hxr_ref[1][:, None, :], pltpu.roll(field(lx - 1), 1, 1))
    beyond = jnp.where(sub == BLOCKS - 1, hxr_ref[0][:, None, :], pltpu.roll(now, BLOCKS - 1, 1))
    u = jnp.zeros(shape, jnp.float32)
    total = jnp.zeros(shape, jnp.float32)
    for g in range(lx):
        after = field(g + 1) if g + 1 < lx else beyond
        to_right = pltpu.roll(now, 1, 2)
        to_left = pltpu.roll(now, LANES - 1, 2)
        column = col_ref[pl.ds(g, BLOCKS, stride=lx), :]
        around = []
        for j in range(tiles):
            for p in range(planes):
                i = j * planes + p
                if j == 0:
                    low = column if p == 0 else pltpu.roll(column, LANES - p, 1)
                else:
                    low = to_right[i - planes]
                if j == tiles - 1:
                    high = pltpu.roll(column, LANES - 1 - planes - p, 1)
                else:
                    high = to_left[i + planes]
                left = jnp.where(lane1 == 0, low, to_right[i])
                right = jnp.where(lane1 == LANES - 1, high, to_left[i])
                under = now[i - 1] if p > 0 else none
                over = now[i + 1] if p < planes - 1 else none
                around.append((over + under) + (left + right))
        around = jnp.stack(around) + (after + before)
        source = now + 0.125 * (around - 6.0 * now)
        m = m_ref[:, pl.ds(g, BLOCKS, stride=lx), :]
        u = (source * m + u) * rx_ref[g]
        total = u if g == 0 else total + ex_ref[g - 1] * u
        ux_ref[g] = u
        before, now = now, after

    def finish_sweep(u, total, nodes, count, length, r_ref, e_ref, u_ref, store, exchange):
        leaves = [leaf_rows(ref, value, count) for ref, value in zip(turns, (u, total))]
        (u_top, a_top), starts = tree_up(nodes, list(zip(*leaves)))
        low, high = exchange(u_top, a_top)
        bounds = tree_down(nodes, starts, low, high)
        low = block_rows(turn0, [b[0] for b in bounds], count)
        value = block_rows(turn1, [b[1] for b in bounds], count)
        for g in range(length - 1, -1, -1):
            value = (u_ref[g] + e_ref[g] * low) + r_ref[g] * value
            store(g, value)

    def exchange_x(u_top, a_top):
        rgx[ix, 0] = u_top
        rgx[ix, 1] = a_top
        send = peers_x(rgx, rsx, rrx)
        for copy in send:
            copy.start()
        started.extend(send)
        for copy in send_cx:
            copy.wait_recv()
        chain = chain_coefficients(cgx, nx)
        for copy in send:
            copy.wait_recv()
        chain_solve(chain, rgx, lastx, firstx, nx)
        return lastx[ix], firstx[ix]

    def exchange_y(u_top, a_top):
        rgy[iy, 0] = u_top
        rgy[iy, 1] = a_top
        send = peers_y(rgy, rsy, rry)
        for copy in send:
            copy.start()
        started.extend(send)
        for copy in send_cy:
            copy.wait_recv()
        chain = chain_coefficients(cgy, ny)
        for copy in send:
            copy.wait_recv()
        chain_solve(chain, rgy, lasty, firsty, ny)
        return lasty[iy], firsty[iy]

    def store_x(g, value):
        mid_ref[:, pl.ds(g, BLOCKS, stride=lx), :] = value

    finish_sweep(u, total, nodes_x, count, lx, rx_ref, ex_ref, ux_ref, store_x, exchange_x)

    for p in range(planes):
        for j in range(tiles):
            midt_ref[p, pl.ds(j * LANES, LANES), :] = mid_ref[j * planes + p].T
    u = jnp.zeros((planes, BLOCKS, LANES), jnp.float32)
    total = u
    for g in range(ly):
        source = midt_ref[:, pl.ds(g, BLOCKS, stride=ly), :]
        m = mt_ref[:, pl.ds(g, BLOCKS, stride=ly), :]
        u = (source * m + u) * ry_ref[g]
        total = u if g == 0 else total + ey_ref[g - 1] * u
        uy_ref[g] = u

    def store_y(g, value):
        midt_ref[:, pl.ds(g, BLOCKS, stride=ly), :] = value

    finish_sweep(u, total, nodes_y, planes, ly, ry_ref, ey_ref, uy_ref, store_y, exchange_y)
    for p in range(planes):
        for j in range(tiles):
            at = pl.ds(j * LANES, LANES)
            out_ref[p, :, at] = midt_ref[p, at, :].T
    for copy, sends, _ in routes:
        pl.when(sends)(copy.wait_send)
    for copy in started:
        copy.wait_send()


def on_device(nx, ny, initial_heat_state, spreading_coefficient):
    planes, rows, columns = initial_heat_state.shape
    count = planes * (columns // LANES)
    lx = rows // BLOCKS
    ly = columns // BLOCKS

    def vmem(*shape):
        return pltpu.VMEM(shape, jnp.float32)

    def dma(number):
        return pltpu.SemaphoreType.DMA((number,))

    return pl.pallas_call(
        functools.partial(kernel, nx, ny),
        out_shape=jax.ShapeDtypeStruct((planes, rows, columns), jnp.float32),
        in_specs=[pl.BlockSpec(memory_space=pltpu.HBM)] * 2,
        out_specs=pl.BlockSpec(memory_space=pltpu.VMEM),
        scratch_shapes=[
            vmem(count, rows, LANES),
            vmem(count, rows, LANES),
            vmem(planes, columns, LANES),
            vmem(lx, count, BLOCKS, LANES),
            vmem(lx, count, BLOCKS, LANES),
            vmem(lx, count, BLOCKS, LANES),
            vmem(ly, planes, BLOCKS, LANES),
            vmem(ly, planes, BLOCKS, LANES),
            vmem(ly, planes, BLOCKS, LANES),
            vmem(count, rows, LANES),
            vmem(planes, columns, LANES),
            vmem(count * BLOCKS, LANES),
            vmem(count * BLOCKS, LANES),
            vmem(count * BLOCKS, LANES),
            vmem(2, count, LANES),
            vmem(2, count, LANES),
            vmem(2, planes, LANES),
            vmem(2, planes, LANES),
            vmem(rows, LANES),
            vmem(nx, 3, count, LANES),
            vmem(nx, 2, count, LANES),
            vmem(ny, 3, planes, LANES),
            vmem(ny, 2, planes, LANES),
            vmem(nx, count, LANES),
            vmem(nx, count, LANES),
            vmem(ny, planes, LANES),
            vmem(ny, planes, LANES),
            dma(2 * (columns // LANES)),
            dma(4),
            dma(4),
            dma(nx - 1),
            dma(nx - 1),
            dma(nx - 1),
            dma(nx - 1),
            dma(ny - 1),
            dma(ny - 1),
            dma(ny - 1),
            dma(ny - 1),
        ],
        compiler_params=pltpu.CompilerParams(
            collective_id=0, has_side_effects=True, vmem_limit_bytes=32 << 20
        ),
    )(
        pltpu.with_memory_space_constraint(initial_heat_state, pltpu.HBM),
        pltpu.with_memory_space_constraint(spreading_coefficient, pltpu.HBM),
    )


def solution(mesh):
    return jax.shard_map(
        functools.partial(on_device, mesh.shape["px"], mesh.shape["py"]),
        mesh=mesh,
        in_specs=(P(None, "px", "py"), P(None, "px", "py")),
        out_specs=P(None, "px", "py"),
        check_vma=False,
    )
```
